512 devices in a mesh: lon: 64 (over y_hi, x, z), mlp: 8 (over y_lo, core).
Axes of the slice: x: 4, y: 8 (y_hi: 2, y_lo: 4; y = y_hi * 4 + y_lo), z: 8, core: 2. Of those that a mesh axis runs over, the one named last changes fastest.
Arguments:
- fields: bfloat16 [48, 1472, 1024], P('mlp', 'lon'), may hold values from -40 to 40
- cotangent: bfloat16 [48, 1472, 1024], P('mlp', 'lon'), may hold values from -6 to 6
- conv_weight: bfloat16 [7, 7, 1024], replicated, may hold values from -0.875 to 0.875
- norm_gain: bfloat16 [1024], replicated, may hold values from 0.099609375 to 1.8984375
- weight_in: bfloat16 [1024, 4096], P(None, 'mlp'), may hold values from -0.1875 to 0.1875
- weight_out: bfloat16 [4096, 1024], P('mlp'), may hold values from -0.09375 to 0.09375
Outputs:
- grad_fields: bfloat16 [48, 1472, 1024], P('mlp', 'lon')
- grad_weight_in: bfloat16 [1024, 4096], P(None, 'mlp')
- grad_weight_out: bfloat16 [4096, 1024], P('mlp')
The draws below stay inside these ranges and needn't reach their ends.
All inputs are finite; a program needn't handle non-finite values.
Results may differ from the reference program's by a relative error of at most 0.0095.
Values may be sent and summed in bfloat16 or wider, within the bound.
A program may use at most 64 MiB of HBM per device.

```python
import math
import jax
import jax.numpy as jnp
import numpy as np
from jax import lax

C = 1024
H = 4096
KS = 7
LON = 1440
SLOTS = 23
LON_SLOTS = 1472
LAT = 48
N_LON = 64
N_MLP = 8


def draw_fields(key, part):
    keys = jax.random.split(key, 3)
    base = jnp.clip(jax.random.normal(keys[0], (LAT, LON_SLOTS, C), jnp.float32), -4.0, 4.0)
    row_scale = jnp.exp(jax.random.uniform(keys[1], (LAT, LON_SLOTS, 1), jnp.float32) * math.log(10.0))
    chan_scale = jnp.exp(jax.random.uniform(keys[2], (1, 1, C), jnp.float32) * math.log(10.0))
    return (base * row_scale * chan_scale * 0.1).astype(jnp.bfloat16)


def block_scale(stream_key, shape, pieces, low, high):
    level = 1.0
    for dim, blocks in pieces:
        heights = jax.random.uniform(jax.random.fold_in(jax.random.fold_in(stream_key, 6), dim), (blocks,), jnp.float32, low / len(pieces), high / len(pieces))
        level = level * jnp.repeat(jnp.exp(heights), shape[dim] // blocks).reshape((-1,) + (1,) * (len(shape) - 1 - dim))
    return level


def scatter_about(rng, dims, scale, bound, cuts=(), kind=jnp.bfloat16):
    entries = scale * jax.random.normal(rng, dims, jnp.float32)
    if cuts:
        entries = entries * block_scale(rng, dims, cuts, -0.22, 0.18)
    return jnp.clip(entries, -bound, bound).astype(kind)


def setup_inputs(seed: int = 0) -> dict:
    streams_of = jax.random.split(jax.random.key(seed), 7)
    return {
        "fields": draw_fields(jax.random.fold_in(streams_of[6], 71), 0),
        "cotangent": scatter_about(streams_of[1], (LAT, LON_SLOTS, C), 1.0, 6.0, ((0, 8), (1, 64))),
        "conv_weight": scatter_about(streams_of[2], (KS, KS, C), (KS * KS) ** -0.5, 0.875),
        "norm_gain": jnp.clip(1.0 + 0.18 * jax.random.normal(streams_of[3], (C,), jnp.float32), 0.099609375, 1.8984375).astype(jnp.bfloat16),
        "weight_in": scatter_about(streams_of[4], (C, H), C ** -0.5, 0.1875, ((1, 8),)),
        "weight_out": scatter_about(streams_of[5], (H, C), H ** -0.5, 0.09375, ((0, 8),)),
    }


def activate(values):
    return values * (0.5 * (1.0 + lax.erf(values * (1.0 / math.sqrt(2.0)))))

def slope(values):
    cumulative = 0.5 * (1.0 + lax.erf(values * (1.0 / math.sqrt(2.0))))
    return cumulative + values * jnp.exp(-0.5 * values * values) * (1.0 / math.sqrt(2.0 * math.pi))

def extend(field, reach):
    padded = jnp.pad(field, ((reach, reach), (0, 0), (0, 0)))
    return jnp.concatenate([padded[:, -reach:], padded, padded[:, :reach]], axis=1)

def live_columns():
    base_count = LON // N_LON
    surplus = LON % N_LON
    chosen = []
    for device in range(N_LON):
        count = base_count + (1 if device < surplus else 0)
        chosen.extend(range(device * SLOTS, device * SLOTS + count))
    return np.array(chosen, dtype=np.int32)

def reference(fields, cotangent, conv_weight, norm_gain, weight_in, weight_out):
    columns = live_columns()
    compact = jnp.take(fields, columns, axis=1)
    cot_compact = jnp.take(cotangent, columns, axis=1)
    lat_all, lon_all, width = compact.shape
    reach = KS // 2
    kernel = conv_weight.astype(jnp.float32)
    padded = extend(compact.astype(jnp.float32), reach)
    mixed = jnp.zeros((lat_all, lon_all, width), jnp.float32)
    for row_off in range(KS):
        for col_off in range(KS):
            mixed = mixed + kernel[row_off, col_off] * padded[row_off:row_off + lat_all, col_off:col_off + lon_all]
    centred = mixed - lax.optimization_barrier(jnp.mean(mixed, axis=-1, keepdims=True))
    inv_std = lax.rsqrt(lax.optimization_barrier(jnp.mean(centred * centred, axis=-1, keepdims=True)) + 1e-06)
    norm_hat = centred * inv_std
    gain = norm_gain.astype(jnp.float32)
    normed = (norm_hat * gain).astype(jnp.bfloat16).reshape(-1, width)
    cot_rows = cot_compact.reshape(-1, width)
    block = H // N_MLP
    grad_normed = jnp.zeros((normed.shape[0], width), jnp.float32)
    grads_in = []
    grads_out = []
    for index in range(N_MLP):
        w_first = weight_in[:, index * block:(index + 1) * block]
        w_second = weight_out[index * block:(index + 1) * block]
        hidden = jnp.dot(normed, w_first, preferred_element_type=jnp.float32)
        activated = activate(hidden).astype(jnp.bfloat16)
        upstream = lax.dot_general(cot_rows, w_second, (((1,), (1,)), ((), ())), preferred_element_type=jnp.float32)
        grad_hidden = (upstream * slope(hidden)).astype(jnp.bfloat16)
        grads_out.append(lax.dot_general(activated, cot_rows, (((0,), (0,)), ((), ())), preferred_element_type=jnp.float32))
        grads_in.append(lax.dot_general(normed, grad_hidden, (((0,), (0,)), ((), ())), preferred_element_type=jnp.float32))
        partial_sum = lax.dot_general(grad_hidden, w_first, (((1,), (1,)), ((), ())), preferred_element_type=jnp.float32)
        rounded = lax.optimization_barrier(partial_sum.astype(jnp.bfloat16))
        grad_normed = grad_normed + rounded.astype(jnp.float32)
    scale = jnp.float32(1.0 / math.sqrt(lat_all * lon_all))
    grad_weight_in = (jnp.concatenate(grads_in, axis=1) * scale).astype(jnp.bfloat16)
    grad_weight_out = (jnp.concatenate(grads_out, axis=0) * scale).astype(jnp.bfloat16)
    scaled = grad_normed.reshape(lat_all, lon_all, width) * gain
    grad_mixed = inv_std * (scaled - lax.optimization_barrier(jnp.mean(scaled, axis=-1, keepdims=True)) - norm_hat * lax.optimization_barrier(jnp.mean(scaled * norm_hat, axis=-1, keepdims=True)))
    grad_mixed = grad_mixed.astype(jnp.bfloat16)
    padded_grad = extend(grad_mixed.astype(jnp.float32), reach)
    result = cot_compact.astype(jnp.float32)
    for row_off in range(KS):
        for col_off in range(KS):
            row_start = 2 * reach - row_off
            col_start = 2 * reach - col_off
            result = result + kernel[row_off, col_off] * padded_grad[row_start:row_start + lat_all, col_start:col_start + lon_all]
    whole = jnp.zeros((lat_all, fields.shape[1], width), jnp.bfloat16)
    whole = whole.at[:, columns].set(result.astype(jnp.bfloat16))
    return (whole, grad_weight_in, grad_weight_out)
```

```python
import math

import jax
import jax.numpy as jnp
from jax import lax
from jax.experimental import pallas as pl
from jax.experimental.pallas import tpu as pltpu
from jax.sharding import PartitionSpec as P

KS = 7
LON = 1440


N_Z, N_X, N_YH = 8, 4, 2
MESH = pl.DeviceIdType.MESH
BF = jnp.bfloat16
F32 = jnp.float32


class Sends:
    def __init__(self, send_sems, recv_sems):
        self.send_sems, self.recv_sems, self.started = send_sems, recv_sems, []

    def start(self, src, dst, device):
        index = len(self.started)
        copy = pltpu.make_async_remote_copy(
            src_ref=src,
            dst_ref=dst,
            send_sem=self.send_sems.at[index],
            recv_sem=self.recv_sems.at[index],
            device_id=device,
            device_id_type=MESH,
        )
        copy.start()
        self.started.append(copy)
        return copy

    def finish(self):
        for copy in self.started:
            copy.wait_send()


def block(ref, start, size):
    return ref.at[pl.ds(pl.multiple_of(start, size), size)]


def ring_reduce(sends, own, stage, recv, me, count, at):
    half = stage.shape[3]
    arrived = {}
    levels = count // 2
    for slot in range(levels):
        for late in (0, 1):
            level = levels - slot - late
            if level < 1:
                continue
            for way in (0, 1):
                sub = way if late == 0 else 1 - way
                step = 1 if way == 0 else -1
                target = lax.rem(me + step * level + count, count)
                value = block(own, target * (2 * half) + sub * half, half)[...]
                before = arrived.get((level + 1, way, sub))
                if before is not None:
                    before.wait_recv()
                    value = value + recv[level, way, sub].astype(F32)
                stage[level - 1, way, sub] = value.astype(BF)
                arrived[level, way, sub] = sends.start(
                    stage.at[level - 1, way, sub],
                    recv.at[level - 1, way, sub],
                    at(lax.rem(me + step + count, count)),
                )
        yield
    for way in (0, 1):
        for sub in (0, 1):
            arrived[1, way, sub].wait_recv()


def ring_gather(sends, out, me, count, at, half):
    arrived = {}
    levels = count // 2
    for level in range(levels):
        for sub in (0, 1):
            for way in (0, 1):
                if level == levels - 1 and sub != way:
                    continue
                step = 1 if way == 0 else -1
                if level > 0:
                    arrived[level - 1, way, sub].wait_recv()
                chunk = lax.rem(me - step * level + count, count)
                rows = block(out, chunk * (2 * half) + sub * half, half)
                arrived[level, way, sub] = sends.start(
                    rows, rows, at(lax.rem(me + step + count, count))
                )
        yield
    for way in (0, 1):
        for sub in (0, 1):
            last = levels - 1 if sub == way else levels - 2
            if last >= 0:
                arrived[last, way, sub].wait_recv()


def ring_sum(own, recv, me, half):
    for sub in (0, 1):
        value = block(own, me * (2 * half) + sub * half, half)[...]
        yield sub, value + recv[0, 0, sub].astype(F32) + recv[0, 1, sub].astype(F32)


def reduce_all(sends, own, out, bufs, ring, line, far, factor):
    stage, recv, flat, pieces, mine, theirs = bufs
    (ring_me, ring_count, ring_at), (line_me, line_count, line_at) = ring, line
    half = stage.shape[3]
    piece = mine.shape[0]
    yield from ring_reduce(sends, own, stage, recv, ring_me, ring_count, ring_at)
    for sub, value in ring_sum(own, recv, ring_me, half):
        flat[pl.ds(sub * half, half)] = value.astype(BF)
    copies = []
    for offset in range(1, line_count):
        target = lax.rem(line_me + offset, line_count)
        copies.append(
            sends.start(block(flat, target * piece, piece), pieces.at[offset - 1], line_at(target))
        )
    yield
    total = block(flat, line_me * piece, piece)[...].astype(F32)
    for offset, copy in enumerate(copies):
        copy.wait_recv()
        total = total + pieces[offset].astype(F32)
    mine[...] = total.astype(BF)
    copy = sends.start(mine, theirs, far)
    yield
    copy.wait_recv()
    total = (mine[...].astype(F32) + theirs[...].astype(F32)) * factor
    place = block(out, ring_me * (2 * half) + line_me * piece, piece)
    place[...] = total.astype(BF)
    copies = []
    for offset in range(1, line_count):
        target = lax.rem(line_me + offset, line_count)
        copies.append(sends.start(place, place, line_at(target)))
    yield
    for copy in copies:
        copy.wait_recv()
    yield from ring_gather(sends, out, ring_me, ring_count, ring_at, half)


def interleave(*parts):
    live = list(parts)
    while live:
        live = [part for part in live if next(part, StopIteration) is not StopIteration]


def reduce_buffers(levels, half, width, line_count):
    piece = 2 * half // line_count
    return [
        pltpu.VMEM((levels, 2, 2, half, width), BF),
        pltpu.VMEM((levels, 2, 2, half, width), BF),
        pltpu.VMEM((2 * half, width), BF),
        pltpu.VMEM((line_count - 1, piece, width), BF),
        pltpu.VMEM((piece, width), BF),
        pltpu.VMEM((piece, width), BF),
    ]


def reduce_kernel(factor, first, second, out_first, out_second, *scratch):
    bufs_first, bufs_second, (send_sems, recv_sems) = scratch[:6], scratch[6:12], scratch[12:]
    lon, mlp = lax.axis_index("lon"), lax.axis_index("mlp")
    z = lax.rem(lon, N_Z)
    x = lax.rem(lax.div(lon, N_Z), N_X)
    high = lax.div(lon, N_X * N_Z)

    def place(far, along_x, along_z):
        return (far * (N_X * N_Z) + along_x * N_Z + along_z, mlp)

    def at_x(other):
        return place(high, other, z)

    def at_z(other):
        return place(high, x, other)

    far = place(1 - high, x, z)
    barrier = pltpu.get_barrier_semaphore()
    peers = [at_z(lax.rem(z + k, N_Z)) for k in range(1, N_Z)]
    peers += [at_x(lax.rem(x + k, N_X)) for k in range(1, N_X)]
    peers.append(far)
    for peer in peers:
        pl.semaphore_signal(barrier, inc=1, device_id=peer, device_id_type=MESH)
    pl.semaphore_wait(barrier, len(peers))
    sends = Sends(send_sems, recv_sems)
    along_x, along_z = (x, N_X, at_x), (z, N_Z, at_z)
    interleave(
        reduce_all(sends, first, out_first, bufs_first, along_z, along_x, far, factor),
        reduce_all(sends, second, out_second, bufs_second, along_x, along_z, far, factor),
    )
    sends.finish()


def reduce_weights(first, second, factor):
    vmem = pl.BlockSpec(memory_space=pltpu.VMEM)
    return pl.pallas_call(
        lambda *refs: reduce_kernel(factor, *refs),
        out_shape=(
            jax.ShapeDtypeStruct(first.shape, BF),
            jax.ShapeDtypeStruct(second.shape, BF),
        ),
        in_specs=[vmem, vmem],
        out_specs=(vmem, vmem),
        scratch_shapes=reduce_buffers(N_Z // 2, 64, first.shape[1], N_X)
        + reduce_buffers(N_X // 2, 64, second.shape[1], N_Z)
        + [pltpu.SemaphoreType.DMA((96,)), pltpu.SemaphoreType.DMA((96,))],
        compiler_params=pltpu.CompilerParams(
            collective_id=0, has_side_effects=True, vmem_limit_bytes=40 << 20
        ),
        name="reduce_weights",
    )(first, second)


def passed_along(value, axis, by):
    count = lax.axis_size(axis)
    return lax.ppermute(value, axis, [(i, (i + by) % count) for i in range(count)])


def with_halo(cells, sides, width):
    for axis, dim in sides:
        count = lax.axis_size(axis)
        ends = count - 1
        head = lax.slice_in_dim(cells, 0, width, axis=dim)
        tail = lax.slice_in_dim(cells, cells.shape[dim] - width, cells.shape[dim], axis=dim)
        cells = jnp.concatenate(
            [
                lax.ppermute(tail, axis, [(i, (i + 1) % count) for i in range(ends)]),
                cells,
                lax.ppermute(head, axis, [((i + 1) % count, i) for i in range(ends)]),
            ],
            axis=dim,
        )
    return cells


def activate(values):
    return values * (0.5 * (1.0 + lax.erf(values * (1.0 / math.sqrt(2.0)))))


def slope(values):
    cumulative = 0.5 * (1.0 + lax.erf(values * (1.0 / math.sqrt(2.0))))
    return cumulative + values * jnp.exp(-0.5 * values * values) * (1.0 / math.sqrt(2.0 * math.pi))


def live_count():
    members = lax.axis_size("lon")
    position = lax.axis_index("lon")
    return LON // members + (position < LON % members).astype(jnp.int32)


def lon_cycle(field, held):
    reach = KS // 2
    first_cols = field[:, :reach]
    last_cols = lax.dynamic_slice_in_dim(field, held - reach, reach, 1)
    from_left = passed_along(last_cols, "lon", 1)
    from_right = passed_along(first_cols, "lon", -1)
    spare = jnp.zeros((field.shape[0], reach, field.shape[2]), field.dtype)
    joined = jnp.concatenate([from_left, field, spare], axis=1)
    return lax.dynamic_update_slice_in_dim(joined, from_right, reach + held, 1)


def extend(field, held):
    reach = KS // 2
    rows = with_halo(field, (("mlp", 0),), reach)
    padded = lon_cycle(rows, held)
    return padded.astype(jnp.float32)


def body(fields, cotangent, conv_weight, norm_gain, weight_in, weight_out):
    lat_dev, slot_count, width = fields.shape
    reach = KS // 2
    held = live_count()
    slot_live = lax.broadcasted_iota(jnp.int32, (1, slot_count, 1), 1) < held
    kernel = conv_weight.astype(jnp.float32)
    padded = extend(fields, held)
    mixed = jnp.zeros((lat_dev, slot_count, width), jnp.float32)
    for row_off in range(KS):
        for col_off in range(KS):
            mixed = (
                mixed
                + kernel[row_off, col_off]
                * padded[row_off : row_off + lat_dev, col_off : col_off + slot_count]
            )
    centred = mixed - jnp.mean(mixed, axis=-1, keepdims=True)
    inv_std = lax.rsqrt(jnp.mean(centred * centred, axis=-1, keepdims=True) + 1e-06)
    norm_hat = centred * inv_std
    gain = norm_gain.astype(jnp.float32)
    normed = jnp.where(slot_live, norm_hat * gain, 0.0).astype(jnp.bfloat16).reshape(-1, width)
    normed_all = lax.all_gather(normed, "mlp", axis=0, tiled=True)
    cot_all = lax.all_gather(cotangent.reshape(-1, width), "mlp", axis=0, tiled=True)
    hidden = jnp.dot(normed_all, weight_in, preferred_element_type=jnp.float32)
    activated = activate(hidden).astype(jnp.bfloat16)
    upstream = lax.dot_general(
        cot_all, weight_out, (((1,), (1,)), ((), ())), preferred_element_type=jnp.float32
    )
    grad_hidden = (upstream * slope(hidden)).astype(jnp.bfloat16)
    grad_second = lax.dot_general(
        activated, cot_all, (((0,), (0,)), ((), ())), preferred_element_type=jnp.float32
    )
    grad_first = lax.dot_general(
        normed_all, grad_hidden, (((0,), (0,)), ((), ())), preferred_element_type=jnp.float32
    )
    grad_normed = lax.psum_scatter(
        lax.dot_general(
            grad_hidden, weight_in, (((1,), (1,)), ((), ())), preferred_element_type=jnp.float32
        ).astype(jnp.bfloat16),
        "mlp",
        scatter_dimension=0,
        tiled=True,
    ).astype(jnp.float32)
    cells = lax.axis_size("mlp") * lat_dev * LON
    out_first, out_second = reduce_weights(grad_first, grad_second, 1.0 / math.sqrt(cells))
    scaled = grad_normed.reshape(lat_dev, slot_count, width) * gain
    grad_mixed = inv_std * (
        scaled
        - jnp.mean(scaled, axis=-1, keepdims=True)
        - norm_hat * jnp.mean(scaled * norm_hat, axis=-1, keepdims=True)
    )
    grad_mixed = grad_mixed.astype(jnp.bfloat16)
    padded_grad = extend(grad_mixed, held)
    result = cotangent.astype(jnp.float32)
    for row_off in range(KS):
        for col_off in range(KS):
            row_start = 2 * reach - row_off
            col_start = 2 * reach - col_off
            result = (
                result
                + kernel[row_off, col_off]
                * padded_grad[row_start : row_start + lat_dev, col_start : col_start + slot_count]
            )
    result = jnp.where(slot_live, result, 0.0)
    return (result.astype(jnp.bfloat16), out_first, out_second)


def solution(mesh):
    in_specs = (
        P("mlp", "lon", None),
        P("mlp", "lon", None),
        P(),
        P(),
        P(None, "mlp"),
        P("mlp", None),
    )
    out_specs = (P("mlp", "lon", None), P(None, "mlp"), P("mlp", None))
    return jax.shard_map(body, mesh=mesh, in_specs=in_specs, out_specs=out_specs, check_vma=False)
```
